32 devices in a mesh: freq: 8 (over y, x, core), rcv: 4 (over z).
Axes of the slice: x: 2, y: 2, z: 4, core: 2. Of those that a mesh axis runs over, the one named last changes fastest.
Arguments:
- kernel: float32 [2, 128, 1024, 1024], P(None, 'freq', 'rcv'), may hold values from -2 to 2, as said below
- focus_start: float32 [8, 1024, 512], P('freq', 'rcv'), may hold values from -6 to 6
- onset: int32 [8, 1024], P('freq', 'rcv'), may hold values from 64 to 447
- freq_order: int32 [128], replicated, may hold values from 0 to 127, each once
Outputs:
- focusing: float32 [8, 1024, 512], P('freq', 'rcv')
- downgoing: float32 [8, 1024, 512], P('freq', 'rcv')
The draws below stay inside these ranges and needn't reach their ends.
Inputs may be any that keep to these rules, and one draw needn't show every extreme that they name: kernel[c,k,s,r] equals kernel[c,k,r,s] exactly (reciprocity).
All inputs are finite; a program needn't handle non-finite values.
Results may differ from the reference program's by a relative error of at most 0.0001.
Values sent between devices are 32-bit elements; how exact they have to be, the bound alone decides.
No kernel may reach another device: no remote copies, remote signals or barrier semaphores. Data moves between devices by JAX's collectives and lax.ppermute only.
A program may use at most 128 MiB of HBM per device.

```python
import math
import jax
import jax.numpy as jnp
from jax import lax

NR = 1024
NT = 512
NF = 128
ITERS = 2
NV = 8


def draw_kernel(key, part):
    full_shape = (2, NF, NR, NR)
    entries = jax.random.truncated_normal(key, -6.0, 6.0, full_shape, jnp.float32)
    return (entries + jnp.swapaxes(entries, 2, 3)) * (0.5 / math.sqrt(NR))


def with_ends(values, key, least, largest):
    longest = values.shape.index(max(values.shape))
    spots = []
    for shift in (0, 1):
        where = [jax.random.randint(jax.random.fold_in(key, axis), (), 0, length) for axis, length in enumerate(values.shape)]
        where[longest] = (where[longest] + shift) % values.shape[longest]
        spots.append(tuple(where))
    return values.at[spots[0]].set(least).at[spots[1]].set(largest)


def block_levels(key, dims, pieces, least, high):
    def one(dim, blocks):
        draws = jax.random.uniform(jax.random.fold_in(jax.random.fold_in(key, 6), dim), (blocks,), jnp.float32, least / len(pieces), high / len(pieces))
        return jnp.repeat(jnp.exp(draws), dims[dim] // blocks).reshape((-1,) + (1,) * (len(dims) - dim - 1))

    gain = one(*pieces[0])
    for cut in pieces[1:]:
        gain = gain * one(*cut)
    return gain


def noise(own_key, extent, deviation, most, cuts=(), kind=jnp.bfloat16):
    drawn = jax.random.normal(own_key, extent, jnp.float32) * deviation
    if len(cuts) > 0:
        drawn = block_levels(own_key, extent, cuts, -0.22, 0.18) * drawn
    return jnp.clip(drawn, min=-most, max=most).astype(kind)


def setup_inputs(seed: int = 0) -> dict:
    streams_of = jax.random.split(jax.random.key(seed), 5)
    kernel = draw_kernel(jax.random.fold_in(streams_of[4], 71), 0)
    focus_start = noise(streams_of[1], (NV, NR, NT), 1.0, 6.0, ((0, 8), (1, 4)), jnp.float32)
    onset = with_ends(jax.random.randint(streams_of[2], (NV, NR), NT // 8, NT - NT // 8), jax.random.fold_in(streams_of[2], 1), NT // 8, (NT - NT // 8) - 1).astype(jnp.int32)
    freq_order = jax.random.permutation(streams_of[3], NF).astype(jnp.int32)
    return dict(kernel=kernel, focus_start=focus_start, onset=onset, freq_order=freq_order)


def make_tables(freq_order, samples):
    sample_ids = jnp.arange(samples, dtype=jnp.int32)
    phase_ids = (freq_order.astype(jnp.int32)[:, None] * sample_ids[None, :]) % samples
    angles = (2.0 * math.pi / samples) * phase_ids.astype(jnp.float32)
    forward = jnp.stack([jnp.cos(angles), -jnp.sin(angles)])
    weights = jnp.where(freq_order == 0, 1.0, 2.0).astype(jnp.float32) / samples
    inverse_operator = forward * weights[None, :, None]
    return forward, inverse_operator


def complex_product(left, right, sign_parity, form):
    real_part = jnp.einsum(form, left[0], right[0], precision=lax.Precision.HIGHEST) - sign_parity * jnp.einsum(form, left[1], right[1], precision=lax.Precision.HIGHEST)
    imag_part = sign_parity * jnp.einsum(form, left[0], right[1], precision=lax.Precision.HIGHEST) + jnp.einsum(form, left[1], right[0], precision=lax.Precision.HIGHEST)
    return jnp.stack([real_part, imag_part])


def reference(kernel, focus_start, onset, freq_order):
    forward, inverse_operator = make_tables(freq_order, NT)
    window_mask = jnp.arange(NT, dtype=jnp.int32)[None, None, :] < onset[:, :, None]

    def convolve(traces, sign_parity):
        spectral_field = jnp.einsum("ckt,vrt->ckvr", forward, traces, precision=lax.Precision.HIGHEST)

        def single_frequency_slice(slot):
            left = lax.dynamic_index_in_dim(spectral_field, slot, 1, keepdims=False)
            right = lax.dynamic_index_in_dim(kernel, slot, 1, keepdims=False)
            return complex_product(left, right, sign_parity, "vr,sr->vs")

        kernel_product = lax.map(single_frequency_slice, jnp.arange(NF, dtype=jnp.int32))
        wavelet_signal = jnp.einsum("ozpn,zoi->pni", kernel_product, inverse_operator, precision=lax.Precision.HIGHEST)
        return jnp.where(window_mask, wavelet_signal, jnp.zeros_like(wavelet_signal))

    focusing = focus_start
    downgoing = focus_start
    for iteration in range(ITERS):
        downgoing = convolve(focusing, 1.0)
        focusing = focus_start + convolve(downgoing, -1.0)
    return focusing, downgoing
```

```python
import functools
import math

import jax
import jax.numpy as jnp
from jax import lax
from jax.experimental import pallas as pl
from jax.experimental.pallas import tpu as pltpu
from jax.sharding import PartitionSpec as P

ITERS = 2
F32, BF16 = jnp.float32, jnp.bfloat16
VMEM = pl.BlockSpec(memory_space=pltpu.VMEM)
ANY = pl.BlockSpec(memory_space=pl.ANY)


def call(body, ins, outs, args, mib, scratch=(), alias=None, flops=0):
    return pl.pallas_call(
        body,
        in_specs=ins,
        out_specs=tuple(VMEM for _ in outs),
        out_shape=tuple(outs),
        scratch_shapes=scratch,
        input_output_aliases=alias or {},
        compiler_params=pltpu.CompilerParams(vmem_limit_bytes=mib << 20),
    )(*args)


def halves(x):
    high = x.astype(BF16)
    return high, (x - high.astype(F32)).astype(BF16)


def dot(a, b, left, right):
    return lax.dot_general(a, b, (((left,), (right,)), ((), ())), preferred_element_type=F32)


def dot3(a, b, left, right):
    return (
        dot(a[0], b[0], left, right) + dot(a[0], b[1], left, right) + dot(a[1], b[0], left, right)
    )


def spectrum_body(table, x, th, tl, out):
    t = halves(table[...])
    th[...] = t[0]
    tl[...] = t[1]
    out[...] = dot3(t, halves(x[...]), 1, 1)


def mute_body(last, add, keep, scale, onset, product, th, tl, *rest):
    rest = list(rest)
    base = rest.pop(0) if add else None
    table = (th[...], tl[...])
    y = dot3(halves((product[...] * scale[...]).T), table, 1, 0)
    t = lax.broadcasted_iota(jnp.int32, y.shape, 1)
    y = jnp.where(t < onset[...], y, 0.0)
    if last:
        rest.pop(0)[...] = base[...] + y if add else y
        return
    if keep:
        rest.pop(0)[...] = y
    s = dot3(table, halves(y), 1, 1)
    rest.pop(0)[...] = s + base[...] if add else s


def hold_body(blocks, kernel, place, high, low, buf, sem):
    n = kernel.shape[1]
    rows = kernel.shape[2]

    def copy(k, slot):
        return pltpu.make_async_copy(kernel.at[:, k], buf.at[slot], sem.at[slot])

    copy(0, 0).start()

    @pl.loop(0, n)
    def _(k):
        slot = lax.rem(k, 2)

        @pl.when(k + 1 < n)
        def _():
            copy(k + 1, 1 - slot).start()

        copy(k, slot).wait()
        for b in range(blocks):
            col = pl.multiple_of(jnp.bitwise_xor(place[0], b) * rows, rows)
            for c in range(2):
                x = buf[slot, c, :, pl.ds(col, rows)]
                h, l = halves(x if b == 0 else x.T)
                high[c, k, pl.ds(b * rows, rows), :] = h
                low[c, k, pl.ds(b * rows, rows), :] = l


def product_body(parity, blocks, first, high, low, *rest):
    fields = rest[: len(blocks)]
    total, out = (None, rest[-1]) if first else (rest[-2], rest[-1])
    _, n, v, rows = out.shape

    def one(k, carry):
        parts = [None, None]
        for b, x in zip(blocks, fields):
            field = jnp.concatenate([x[0, k], x[1, k]], axis=0)
            h, l = halves(field)
            both = jnp.concatenate([h, l], axis=0)
            for c in range(2):
                p = dot(both, high[c, k, pl.ds(b * rows, rows), :], 1, 0)
                p = p[: 2 * v] + p[2 * v :] + dot(h, low[c, k, pl.ds(b * rows, rows), :], 1, 0)
                parts[c] = p if parts[c] is None else parts[c] + p
        re = parts[0][:v] - parity * parts[1][v:]
        im = parity * parts[1][:v] + parts[0][v:]
        out[0, k] = re if first else total[0, k] + re
        out[1, k] = im if first else total[1, k] + im
        return carry

    lax.fori_loop(0, n, one, 0, unroll=2 if n % 2 == 0 else 1)


def body(z_size, groups, kernel, focus_start, onset, freq_order):
    sds = jax.ShapeDtypeStruct
    _, n, rows, receivers = kernel.shape
    own, samples = focus_start.shape[0], focus_start.shape[2]
    n_f = freq_order.shape[0] // n
    points = n_f * own
    place = lax.axis_index("rcv")[None].astype(jnp.int32)

    order = jnp.broadcast_to(freq_order.reshape(n_f, 1, n), (n_f, 2, n)).reshape(-1)
    part = jnp.broadcast_to(jnp.arange(2).reshape(1, 2, 1), (n_f, 2, n)).reshape(-1)
    phase = order[:, None] * jnp.arange(samples, dtype=jnp.int32)[None, :] % samples
    angle = 2.0 * math.pi / samples * phase.astype(F32)
    table = jnp.where(part[:, None] == 0, jnp.cos(angle), -jnp.sin(angle))
    scale = (jnp.where(order == 0, 1.0, 2.0).astype(F32) / samples)[:, None]
    n_rows = 2 * freq_order.shape[0]

    traces = focus_start.reshape(own * rows, samples)
    limit = onset.reshape(own * rows, 1)
    th, tl, start = call(
        spectrum_body,
        [VMEM] * 2,
        [sds((n_rows, samples), BF16)] * 2 + [sds((n_rows, own * rows), F32)],
        (table, traces),
        16,
    )

    held = None

    def product(spectrum, parity):
        nonlocal held
        s = spectrum.reshape(n_f, 2 * n, own, rows)
        x = lax.all_to_all(s, "freq", split_axis=0, concat_axis=0, tiled=True)
        x = x.reshape(n_f, 2, n, own, rows).transpose(1, 2, 0, 3, 4).reshape(2, n, points, rows)
        far = [x] + [
            lax.ppermute(x, "rcv", [(i, i ^ d) for i in range(z_size)]) for d in range(1, z_size)
        ]
        if held is None:
            shape = (2, n, receivers, rows)
            held = pl.pallas_call(
                functools.partial(hold_body, z_size),
                in_specs=[ANY, pl.BlockSpec(memory_space=pltpu.SMEM)],
                out_specs=(VMEM, VMEM),
                out_shape=(pltpu.VMEM(shape, BF16), pltpu.VMEM(shape, BF16)),
                scratch_shapes=[
                    pltpu.VMEM((2, 2, rows, receivers), F32),
                    pltpu.SemaphoreType.DMA((2,)),
                ],
                compiler_params=pltpu.CompilerParams(vmem_limit_bytes=16 << 20),
            )(kernel, place)
        total = None
        for blocks in groups:
            args = (*held, *[far[b] for b in blocks])
            first = total is None
            if not first:
                args = (*args, total)
            (total,) = call(
                functools.partial(product_body, parity, blocks, first),
                [VMEM] * len(args),
                [sds((2, n, points, rows), F32)],
                args,
                12,
                alias=None if first else {len(args) - 1: 0},
            )
        back = total.reshape(2 * n, n_f, own, rows).transpose(1, 0, 2, 3)
        back = lax.all_to_all(back, "freq", split_axis=0, concat_axis=0, tiled=True)
        return back.reshape(n_rows, own * rows)

    def mute(back, last, add, keep):
        outs = [sds((own * rows, samples), F32)] if last or keep else []
        outs += [] if last else [sds((n_rows, own * rows), F32)]
        args = (scale, limit, back, th, tl)
        if add:
            args = (*args, traces if last else start)
        got = call(
            functools.partial(mute_body, last, add, keep), [VMEM] * len(args), outs, args, 16
        )
        return got

    field = start
    for iteration in range(ITERS):
        final = iteration == ITERS - 1
        got = mute(product(field, 1.0), False, False, final)
        downgoing, field = got if final else (None, got[0])
        got = mute(product(field, -1.0), final, True, False)
        field = got[0]
    return field.reshape(focus_start.shape), downgoing.reshape(focus_start.shape)


def solution(mesh):
    in_specs = (P(None, "freq", "rcv", None), P("freq", "rcv", None), P("freq", "rcv"), P())
    out_specs = (P("freq", "rcv", None), P("freq", "rcv", None))
    z_size = mesh.shape["rcv"]
    groups = [[b] for b in range(z_size)]
    return jax.shard_map(
        functools.partial(body, z_size, groups),
        mesh=mesh,
        in_specs=in_specs,
        out_specs=out_specs,
        check_vma=False,
    )
```

```python
import functools
import math

import jax
import jax.numpy as jnp
from jax import lax
from jax.experimental import pallas as pl
from jax.experimental.pallas import tpu as pltpu
from jax.sharding import PartitionSpec as P

ITERS = 2
F32, BF16 = jnp.float32, jnp.bfloat16
VMEM = pl.BlockSpec(memory_space=pltpu.VMEM)
ANY = pl.BlockSpec(memory_space=pl.ANY)


def call(body, ins, outs, args, mib, alias=None):
    return pl.pallas_call(
        body,
        in_specs=ins,
        out_specs=tuple(VMEM for _ in outs),
        out_shape=tuple(outs),
        input_output_aliases=alias or {},
        compiler_params=pltpu.CompilerParams(vmem_limit_bytes=mib << 20),
    )(*args)


def halves(x):
    high = x.astype(BF16)
    return high, (x - high.astype(F32)).astype(BF16)


def dot(a, b, left, right):
    return lax.dot_general(a, b, (((left,), (right,)), ((), ())), preferred_element_type=F32)


def dot3(a, b, left, right):
    return (
        dot(a[0], b[0], left, right) + dot(a[0], b[1], left, right) + dot(a[1], b[0], left, right)
    )


def column(row, length, stride):
    shape = (length, row.shape[1])
    hit = lax.broadcasted_iota(jnp.int32, shape, 0) // stride
    hit = hit == lax.broadcasted_iota(jnp.int32, shape, 1)
    return jnp.sum(jnp.where(hit, row.astype(F32), 0.0), axis=1, keepdims=True)


def spectrum_body(order, onset, x, th, tl, scale, limit, out):
    rows, samples = th.shape
    q = column(order[...], rows, 2)
    scale[...] = jnp.where(q == 0.0, 1.0, 2.0) / samples
    limit[...] = column(onset[...], limit.shape[0], 1).astype(jnp.int32)
    part = lax.broadcasted_iota(jnp.int32, (rows, samples), 0) & 1
    time = lax.broadcasted_iota(jnp.int32, (rows, samples), 1)
    phase = lax.rem(q.astype(jnp.int32) * time + part * (samples // 4), samples)
    table = halves(jnp.cos(2.0 * math.pi / samples * phase.astype(F32)))
    th[...] = table[0]
    tl[...] = table[1]
    out[...] = dot3(table, halves(x[...]), 1, 1)


def mute_body(last, add, keep, scale, onset, product, th, tl, *rest):
    rest = list(rest)
    base = rest.pop(0) if add else None
    table = (th[...], tl[...])
    y = dot3(halves((product[...] * scale[...]).T), table, 1, 0)
    t = lax.broadcasted_iota(jnp.int32, y.shape, 1)
    y = jnp.where(t < onset[...], y, 0.0)
    if last:
        rest.pop(0)[...] = base[...] + y if add else y
        return
    if keep:
        rest.pop(0)[...] = y
    s = dot3(table, halves(y), 1, 1)
    rest.pop(0)[...] = s + base[...] if add else s


def hold_body(blocks, kernel, place, *rest):
    *outs, buf, sem = rest
    n = kernel.shape[1]
    rows = kernel.shape[2]

    def copy(k, slot):
        return pltpu.make_async_copy(kernel.at[:, k], buf.at[slot], sem.at[slot])

    copy(0, 0).start()

    @pl.loop(0, n)
    def _(k):
        slot = lax.rem(k, 2)

        @pl.when(k + 1 < n)
        def _():
            copy(k + 1, 1 - slot).start()

        copy(k, slot).wait()
        for b in range(blocks):
            col = pl.multiple_of(jnp.bitwise_xor(place[0], b) * rows, rows)
            for c in range(2):
                x = buf[slot, c, :, pl.ds(col, rows)]
                h, l = halves(x if b == 0 else x.T)
                outs[2 * b][c, k] = h
                outs[2 * b + 1][c, k] = l


def product_body(parity, pieces, first, *rest):
    highs, lows = rest[: len(pieces)], rest[len(pieces) : 2 * len(pieces)]
    fields = rest[2 * len(pieces) : 3 * len(pieces)]
    total, out = (None, rest[-1]) if first else (rest[-2], rest[-1])
    v, rows = out.shape[2:]
    spans = sorted({(at, at + x.shape[0]) for (_, at), x in zip(pieces, fields)})
    cuts = sorted({end for span in spans for end in span})

    def one(k, here):
        parts = [None, None]
        for high, low, at, x in here:
            h, l = halves(x[k - at].reshape(2 * v, rows))
            both = jnp.concatenate([h, l], axis=0)
            for c in range(2):
                p = dot(both, high[c, k], 1, 0)
                p = p[: 2 * v] + p[2 * v :] + dot(h, low[c, k], 1, 0)
                parts[c] = p if parts[c] is None else parts[c] + p
        re = parts[0][:v] - parity * parts[1][v:]
        im = parity * parts[1][:v] + parts[0][v:]
        out[k, 0] = re if first else total[k, 0] + re
        out[k, 1] = im if first else total[k, 1] + im

    for begin, end in zip(cuts[:-1], cuts[1:]):
        here = [
            (high, low, at, x)
            for (_, at), high, low, x in zip(pieces, highs, lows, fields)
            if at <= begin and end <= at + x.shape[0]
        ]
        if not here:
            continue
        step = math.gcd(end - begin, max(1, 8 // len(here)))

        @pl.loop(begin // step, end // step)
        def _(i):
            for j in range(step):
                one(i * step + j, here)


def body(z_size, kernel, focus_start, onset, freq_order):
    sds = jax.ShapeDtypeStruct
    _, n, rows, receivers = kernel.shape
    own, samples = focus_start.shape[0], focus_start.shape[2]
    n_f = freq_order.shape[0] // n
    points = n_f * own
    place = lax.axis_index("rcv")[None].astype(jnp.int32)

    n_rows = 2 * freq_order.shape[0]
    traces = focus_start.reshape(own * rows, samples)
    th, tl, scale, limit, start = call(
        spectrum_body,
        [VMEM] * 3,
        [sds((n_rows, samples), BF16)] * 2
        + [sds((n_rows, 1), F32), sds((own * rows, 1), jnp.int32), sds((n_rows, own * rows), F32)],
        (freq_order.reshape(1, -1), onset.reshape(1, -1), traces),
        8,
    )

    held = None

    def shift(x, d):
        return lax.ppermute(x, "rcv", [(i, i ^ d) for i in range(z_size)])

    def gather(x):
        half = n // 2
        if z_size != 4 or n % 2:
            return [[(d, 0, shift(x, d) if d else x)] for d in range(z_size)]
        low, high = x[:half], x[half:]
        b0 = shift(low, 2)
        c1 = shift(high, 3)
        b1 = shift(high, 2)
        a = shift(x, 1)
        c0 = shift(b0, 1)
        return [[(0, 0, x)], [(2, 0, b0), (3, half, c1)], [(2, half, b1), (1, 0, a)], [(3, 0, c0)]]

    def product(spectrum, parity):
        nonlocal held
        s = spectrum.reshape(n_f, 2 * n, own, rows)
        x = lax.all_to_all(s, "freq", split_axis=0, concat_axis=0, tiled=True)
        x = x.reshape(n_f, n, 2, own, rows).transpose(1, 2, 0, 3, 4).reshape(n, 2, points, rows)
        groups = gather(x)
        if held is None:
            shape = (2, n, rows, rows)
            held = pl.pallas_call(
                functools.partial(hold_body, z_size),
                in_specs=[ANY, pl.BlockSpec(memory_space=pltpu.SMEM)],
                out_specs=(VMEM,) * (2 * z_size),
                out_shape=(pltpu.VMEM(shape, BF16),) * (2 * z_size),
                scratch_shapes=[
                    pltpu.VMEM((2, 2, rows, receivers), F32),
                    pltpu.SemaphoreType.DMA((2,)),
                ],
                compiler_params=pltpu.CompilerParams(vmem_limit_bytes=9 << 20),
            )(kernel, place)
        total = None
        for group in groups:
            args = [held[2 * b + h] for h in (0, 1) for b, _, _ in group]
            args += [field for _, _, field in group]
            first = total is None
            if not first:
                args.append(total)
            (total,) = call(
                functools.partial(product_body, parity, [piece[:2] for piece in group], first),
                [VMEM] * len(args),
                [sds((n, 2, points, rows), F32)],
                args,
                8,
                alias=None if first else {len(args) - 1: 0},
            )
        back = total.reshape(2 * n, n_f, own, rows).transpose(1, 0, 2, 3)
        back = lax.all_to_all(back, "freq", split_axis=0, concat_axis=0, tiled=True)
        return back.reshape(n_rows, own * rows)

    def mute(back, last, add, keep):
        outs = [sds((own * rows, samples), F32)] if last or keep else []
        outs += [] if last else [sds((n_rows, own * rows), F32)]
        args = (scale, limit, back, th, tl)
        if add:
            args = (*args, traces if last else start)
        got = call(
            functools.partial(mute_body, last, add, keep), [VMEM] * len(args), outs, args, 8
        )
        return got

    field = start
    for iteration in range(ITERS):
        final = iteration == ITERS - 1
        got = mute(product(field, 1.0), False, False, final)
        downgoing, field = got if final else (None, got[0])
        got = mute(product(field, -1.0), final, True, False)
        field = got[0]
    return field.reshape(focus_start.shape), downgoing.reshape(focus_start.shape)


def solution(mesh):
    in_specs = (P(None, "freq", "rcv", None), P("freq", "rcv", None), P("freq", "rcv"), P())
    out_specs = (P("freq", "rcv", None), P("freq", "rcv", None))
    z_size = mesh.shape["rcv"]
    return jax.shard_map(
        functools.partial(body, z_size),
        mesh=mesh,
        in_specs=in_specs,
        out_specs=out_specs,
        check_vma=False,
    )
```

```python
import functools
import math

import jax
import jax.numpy as jnp
from jax import lax
from jax.experimental import pallas as pl
from jax.experimental.pallas import tpu as pltpu
from jax.sharding import PartitionSpec as P


ITERS = 2
F32, BF16 = jnp.float32, jnp.bfloat16
VMEM = pl.BlockSpec(memory_space=pltpu.VMEM)
HBM = pl.BlockSpec(memory_space=pltpu.HBM)


def call(body, ins, outs, args, mib=8, alias=None, scratch=()):
    return pl.pallas_call(
        body,
        in_specs=ins,
        out_specs=tuple(VMEM for _ in outs),
        out_shape=tuple(outs),
        scratch_shapes=scratch,
        input_output_aliases=alias or {},
        compiler_params=pltpu.CompilerParams(vmem_limit_bytes=mib << 20),
    )(*args)


def halves(x):
    high = x.astype(BF16)
    return high, (x - high.astype(F32)).astype(BF16)


def dot(a, b, left, right):
    return lax.dot_general(a, b, (((left,), (right,)), ((), ())), preferred_element_type=F32)


def dot3(a, b, left, right):
    return (
        dot(a[0], b[0], left, right) + dot(a[0], b[1], left, right) + dot(a[1], b[0], left, right)
    )


def column(row, length, stride):
    shape = (length, row.shape[1])
    hit = lax.broadcasted_iota(jnp.int32, shape, 0) // stride
    hit = hit == lax.broadcasted_iota(jnp.int32, shape, 1)
    return jnp.sum(jnp.where(hit, row.astype(F32), 0.0), axis=1, keepdims=True)


def cosine(turn):
    x = (2.0 * math.pi) * (0.25 - jnp.minimum(turn, 1.0 - turn))
    square = x * x
    series = 0.0
    for power in range(13, 0, -2):
        series = series * square + (-1.0) ** (power // 2) / math.factorial(power)
    return series * x


def spectrum_body(order_in, onset_in, x_in, th, tl, scale, limit, out, order, onset, x, sems):
    pairs = ((order_in, order), (onset_in, onset), (x_in, x))
    copies = [pltpu.make_async_copy(a, b, sems.at[i]) for i, (a, b) in enumerate(pairs)]
    for copy in copies:
        copy.start()
    rows, samples = th.shape
    shape = (rows, samples)
    time = lax.broadcasted_iota(jnp.int32, shape, 1).astype(F32) / samples
    part = (lax.broadcasted_iota(jnp.int32, shape, 0) & 1).astype(F32) * 0.25
    copies[0].wait()
    q = column(order[...], rows, 2)
    scale[...] = jnp.where(q == 0.0, 1.0, 2.0) / samples
    turn = q * time + part
    table = halves(cosine(turn - jnp.floor(turn)))
    th[...] = table[0]
    tl[...] = table[1]
    copies[1].wait()
    limit[...] = column(onset[...], limit.shape[0], 1).astype(jnp.int32)
    copies[2].wait()
    out[...] = dot3(table, halves(x[...]), 1, 1)


def mute_body(last, add, scale, onset, product, th, tl, *rest):
    table = (th[...], tl[...])
    y = dot3(halves((product[...] * scale[...]).T), table, 1, 0)
    t = lax.broadcasted_iota(jnp.int32, y.shape, 1)
    y = jnp.where(t < onset[...], y, 0.0)
    if not last:
        y = dot3(table, halves(y), 1, 1)
    rest[-1][...] = rest[0][...] + y if add else y


def hold_body(blocks, kernel, place, *rest):
    *outs, buf, sem = rest
    n = kernel.shape[1]
    rows = kernel.shape[2]

    def copy(k, slot):
        return pltpu.make_async_copy(kernel.at[:, k], buf.at[slot], sem.at[slot])

    copy(0, 0).start()

    @pl.loop(0, n)
    def _(k):
        slot = lax.rem(k, 2)

        @pl.when(k + 1 < n)
        def _():
            copy(k + 1, 1 - slot).start()

        copy(k, slot).wait()
        for b in range(blocks):
            col = pl.multiple_of(jnp.bitwise_xor(place[0], b) * rows, rows)
            for c in range(2):
                x = buf[slot, c, :, pl.ds(col, rows)]
                h, l = halves(x if b == 0 else x.T)
                outs[2 * b][c, k] = h
                outs[2 * b + 1][c, k] = l


def product_body(parity, pieces, first, *rest):
    highs, lows = rest[: len(pieces)], rest[len(pieces) : 2 * len(pieces)]
    fields = rest[2 * len(pieces) : 3 * len(pieces)]
    total, out = (None, rest[-1]) if first else (rest[-2], rest[-1])
    v, rows = out.shape[2:]
    spans = sorted({(at, at + x.shape[0]) for (_, at), x in zip(pieces, fields)})
    cuts = sorted({end for span in spans for end in span})

    def one(k, here):
        parts = [None, None]
        for high, low, at, x in here:
            h, l = halves(x[k - at].reshape(2 * v, rows))
            both = jnp.concatenate([h, l], axis=0)
            for c in range(2):
                p = dot(both, high[c, k], 1, 0)
                p = p[: 2 * v] + p[2 * v :] + dot(h, low[c, k], 1, 0)
                parts[c] = p if parts[c] is None else parts[c] + p
        re = parts[0][:v] - parity * parts[1][v:]
        im = parity * parts[1][:v] + parts[0][v:]
        out[k, 0] = re if first else total[k, 0] + re
        out[k, 1] = im if first else total[k, 1] + im

    for begin, end in zip(cuts[:-1], cuts[1:]):
        here = [
            (high, low, at, x)
            for (_, at), high, low, x in zip(pieces, highs, lows, fields)
            if at <= begin and end <= at + x.shape[0]
        ]
        if not here:
            continue
        step = math.gcd(end - begin, max(1, 8 // len(here)))

        @pl.loop(begin // step, end // step)
        def _(i):
            for j in range(step):
                one(i * step + j, here)


def body(z_size, kernel, focus_start, onset, freq_order):
    sds = jax.ShapeDtypeStruct
    _, n, rows, receivers = kernel.shape
    own, samples = focus_start.shape[0], focus_start.shape[2]
    n_f = freq_order.shape[0] // n
    points = n_f * own
    place = lax.axis_index("rcv")[None].astype(jnp.int32)

    n_rows = 2 * freq_order.shape[0]
    traces = focus_start.reshape(own * rows, samples)
    th, tl, scale, limit, start = call(
        spectrum_body,
        [HBM] * 3,
        [sds((n_rows, samples), BF16)] * 2
        + [sds((n_rows, 1), F32), sds((own * rows, 1), jnp.int32), sds((n_rows, own * rows), F32)],
        (freq_order.reshape(1, -1), onset.reshape(1, -1), traces),
        scratch=[
            pltpu.VMEM((1, n_rows // 2), jnp.int32),
            pltpu.VMEM((1, own * rows), jnp.int32),
            pltpu.VMEM((own * rows, samples), F32),
            pltpu.SemaphoreType.DMA((3,)),
        ],
    )

    held = None

    def shift(x, d):
        return lax.ppermute(x, "rcv", [(i, i ^ d) for i in range(z_size)])

    def gather(x, relay):
        half = n // 2
        if z_size != 4 or n % 2 or not relay:
            return [[(0, 0, x)]] + [[(d, 0, shift(x, d))] for d in range(1, z_size)]
        low, high = x[:half], x[half:]
        b0 = shift(low, 2)
        c1 = shift(high, 3)
        b1 = shift(high, 2)
        a = shift(x, 1)
        c0 = shift(b0, 1)
        return [[(0, 0, x)], [(2, 0, b0), (3, half, c1)], [(2, half, b1), (1, 0, a)], [(3, 0, c0)]]

    def product(spectrum, parity):
        nonlocal held
        s = spectrum.reshape(n_f, 2 * n, own, rows)
        x = lax.all_to_all(s, "freq", split_axis=0, concat_axis=0, tiled=True)
        x = x.reshape(n_f, n, 2, own, rows).transpose(1, 2, 0, 3, 4).reshape(n, 2, points, rows)
        groups = gather(x, held is not None)
        if held is None:
            shape = (2, n, rows, rows)
            held = pl.pallas_call(
                functools.partial(hold_body, z_size),
                in_specs=[HBM, pl.BlockSpec(memory_space=pltpu.SMEM)],
                out_specs=(VMEM,) * (2 * z_size),
                out_shape=(pltpu.VMEM(shape, BF16),) * (2 * z_size),
                scratch_shapes=[
                    pltpu.VMEM((2, 2, rows, receivers), F32),
                    pltpu.SemaphoreType.DMA((2,)),
                ],
                compiler_params=pltpu.CompilerParams(vmem_limit_bytes=9 << 20),
            )(kernel, place)
        total = None
        for group in groups:
            args = [held[2 * b + h] for h in (0, 1) for b, _, _ in group]
            args += [field for _, _, field in group]
            first = total is None
            if not first:
                args.append(total)
            (total,) = call(
                functools.partial(product_body, parity, [piece[:2] for piece in group], first),
                [VMEM] * len(args),
                [sds((n, 2, points, rows), F32)],
                args,
                alias=None if first else {len(args) - 1: 0},
            )
        back = total.reshape(2 * n, n_f, own, rows).transpose(1, 0, 2, 3)
        back = lax.all_to_all(back, "freq", split_axis=0, concat_axis=0, tiled=True)
        return back.reshape(n_rows, own * rows)

    def mute(back, last, base):
        outs = [sds((own * rows, samples) if last else (n_rows, own * rows), F32)]
        args = (scale, limit, back, th, tl) + (() if base is None else (base,))
        body = functools.partial(mute_body, last, base is not None)
        return call(body, [VMEM] * len(args), outs, args)[0]

    field = start
    for iteration in range(ITERS):
        final = iteration == ITERS - 1
        back = product(field, 1.0)
        field = mute(back, False, None)
        if final:
            downgoing = mute(back, True, None)
        back = product(field, -1.0)
        field = mute(back, final, traces if final else start)
    return field.reshape(focus_start.shape), downgoing.reshape(focus_start.shape)


def solution(mesh):
    in_specs = (P(None, "freq", "rcv", None), P("freq", "rcv", None), P("freq", "rcv"), P())
    out_specs = (P("freq", "rcv", None), P("freq", "rcv", None))
    return jax.shard_map(
        functools.partial(body, mesh.shape["rcv"]),
        mesh=mesh,
        in_specs=in_specs,
        out_specs=out_specs,
        check_vma=False,
    )
```

```python
import functools
import math

import jax
import jax.numpy as jnp
from jax import lax
from jax.experimental import pallas as pl
from jax.experimental.pallas import tpu as pltpu
from jax.sharding import PartitionSpec as P


ITERS = 2
F32, BF16 = jnp.float32, jnp.bfloat16
VMEM = pl.BlockSpec(memory_space=pltpu.VMEM)
HBM = pl.BlockSpec(memory_space=pltpu.HBM)


def call(body, ins, outs, args, mib=8, alias=None, scratch=()):
    return pl.pallas_call(
        body,
        in_specs=ins,
        out_specs=tuple(VMEM for _ in outs),
        out_shape=tuple(outs),
        scratch_shapes=scratch,
        input_output_aliases=alias or {},
        compiler_params=pltpu.CompilerParams(vmem_limit_bytes=mib << 20),
    )(*args)


def halves(x):
    high = x.astype(BF16)
    return high, (x - high.astype(F32)).astype(BF16)


def dot(a, b, left, right):
    return lax.dot_general(a, b, (((left,), (right,)), ((), ())), preferred_element_type=F32)


def dot3(a, b, left, right):
    return (
        dot(a[0], b[0], left, right) + dot(a[0], b[1], left, right) + dot(a[1], b[0], left, right)
    )


def column(row, length, stride):
    shape = (length, row.shape[1])
    hit = lax.broadcasted_iota(jnp.int32, shape, 0) // stride
    hit = hit == lax.broadcasted_iota(jnp.int32, shape, 1)
    return jnp.sum(jnp.where(hit, row.astype(F32), 0.0), axis=1, keepdims=True)


def cosine(turn):
    x = (2.0 * math.pi) * (0.25 - jnp.minimum(turn, 1.0 - turn))
    square = x * x
    series = 0.0
    for power in range(13, 0, -2):
        series = series * square + (-1.0) ** (power // 2) / math.factorial(power)
    return series * x


def spectrum_body(order_in, onset_in, x_in, th, tl, scale, limit, out, order, onset, x, sems):
    pairs = ((order_in, order), (onset_in, onset), (x_in, x))
    copies = [pltpu.make_async_copy(a, b, sems.at[i]) for i, (a, b) in enumerate(pairs)]
    for copy in copies:
        copy.start()
    rows, samples = th.shape
    shape = (rows, samples)
    time = lax.broadcasted_iota(jnp.int32, shape, 1).astype(F32) / samples
    part = (lax.broadcasted_iota(jnp.int32, shape, 0) & 1).astype(F32) * 0.25
    copies[0].wait()
    q = column(order[...], rows, 2)
    scale[...] = jnp.where(q == 0.0, 1.0, 2.0) / samples
    turn = q * time + part
    table = halves(cosine(turn - jnp.floor(turn)))
    th[...] = table[0]
    tl[...] = table[1]
    copies[1].wait()
    limit[...] = column(onset[...], limit.shape[0], 1).astype(jnp.int32)
    copies[2].wait()
    out[...] = dot3(table, halves(x[...]), 1, 1)


def mute_body(last, add, scale, onset, product, th, tl, *rest):
    table = (th[...], tl[...])
    y = dot3(halves((product[...] * scale[...]).T), table, 1, 0)
    t = lax.broadcasted_iota(jnp.int32, y.shape, 1)
    y = jnp.where(t < onset[...], y, 0.0)
    if not last:
        y = dot3(table, halves(y), 1, 1)
    rest[-1][...] = rest[0][...] + y if add else y


def hold_body(blocks, kernel, place, *rest):
    *outs, buf, sem = rest
    n, rows = kernel.shape[1:3]
    slots = buf.shape[0]

    def copy(k):
        slot = lax.rem(k, slots)
        return pltpu.make_async_copy(kernel.at[:, k], buf.at[slot], sem.at[slot])

    for k in range(min(slots - 1, n)):
        copy(k).start()

    @pl.loop(0, n)
    def _(k):
        @pl.when(k + slots - 1 < n)
        def _():
            copy(k + slots - 1).start()

        copy(k).wait()
        slot = lax.rem(k, slots)
        for b in range(blocks):
            col = pl.multiple_of(jnp.bitwise_xor(place[0], b) * rows, rows)
            for c in range(2):
                x = buf[slot, c, :, pl.ds(col, rows)]
                h, l = halves(x if b == 0 else x.T)
                outs[2 * b][c, k] = h
                outs[2 * b + 1][c, k] = l


def product_body(parity, pieces, first, *rest):
    highs, lows = rest[: len(pieces)], rest[len(pieces) : 2 * len(pieces)]
    fields = rest[2 * len(pieces) : 3 * len(pieces)]
    total, out = (None, rest[-1]) if first else (rest[-2], rest[-1])
    v, rows = out.shape[2:]
    spans = sorted({(at, at + x.shape[0]) for (_, at), x in zip(pieces, fields)})
    cuts = sorted({end for span in spans for end in span})

    def one(k, here):
        parts = [None, None]
        for high, low, at, x in here:
            h, l = halves(x[k - at].reshape(2 * v, rows))
            both = jnp.concatenate([h, l], axis=0)
            for c in range(2):
                p = dot(both, high[c, k], 1, 0)
                p = p[: 2 * v] + p[2 * v :] + dot(h, low[c, k], 1, 0)
                parts[c] = p if parts[c] is None else parts[c] + p
        re = parts[0][:v] - parity * parts[1][v:]
        im = parity * parts[1][:v] + parts[0][v:]
        out[k, 0] = re if first else total[k, 0] + re
        out[k, 1] = im if first else total[k, 1] + im

    for begin, end in zip(cuts[:-1], cuts[1:]):
        here = [
            (high, low, at, x)
            for (_, at), high, low, x in zip(pieces, highs, lows, fields)
            if at <= begin and end <= at + x.shape[0]
        ]
        if not here:
            continue
        step = math.gcd(end - begin, max(1, 8 // len(here)))

        @pl.loop(begin // step, end // step)
        def _(i):
            for j in range(step):
                one(i * step + j, here)


def body(z_size, kernel, focus_start, onset, freq_order):
    sds = jax.ShapeDtypeStruct
    _, n, rows, receivers = kernel.shape
    own, samples = focus_start.shape[0], focus_start.shape[2]
    n_f = freq_order.shape[0] // n
    points = n_f * own
    place = lax.axis_index("rcv")[None].astype(jnp.int32)

    n_rows = 2 * freq_order.shape[0]
    traces = focus_start.reshape(own * rows, samples)
    th, tl, scale, limit, start = call(
        spectrum_body,
        [HBM] * 3,
        [sds((n_rows, samples), BF16)] * 2
        + [sds((n_rows, 1), F32), sds((own * rows, 1), jnp.int32), sds((n_rows, own * rows), F32)],
        [
            pltpu.with_memory_space_constraint(x, pltpu.HBM)
            for x in (freq_order.reshape(1, -1), onset.reshape(1, -1), traces)
        ],
        scratch=[
            pltpu.VMEM((1, n_rows // 2), jnp.int32),
            pltpu.VMEM((1, own * rows), jnp.int32),
            pltpu.VMEM((own * rows, samples), F32),
            pltpu.SemaphoreType.DMA((3,)),
        ],
    )

    held = None

    def shift(x, d):
        return lax.ppermute(x, "rcv", [(i, i ^ d) for i in range(z_size)])

    def gather(x):
        half = n // 2
        if z_size != 4 or n % 2:
            return [[(0, 0, x)]] + [[(d, 0, shift(x, d))] for d in range(1, z_size)]
        low, high = x[:half], x[half:]
        b0 = shift(low, 2)
        a = shift(x, 1)
        c1 = shift(high, 3)
        b1 = shift(high, 2)
        c0 = shift(b0, 1)
        groups = [[(0, 0, x)], [(2, 0, b0)], [(3, half, c1)]]
        late = [[(1, 0, a)], [(2, half, b1)]]
        relayed = [[(3, 0, c0)]]
        return groups + (late + relayed if held is None else relayed + late)

    def hold():
        shape = (2, n, rows, rows)
        return pl.pallas_call(
            functools.partial(hold_body, z_size),
            in_specs=[HBM, pl.BlockSpec(memory_space=pltpu.SMEM)],
            out_specs=(VMEM,) * (2 * z_size),
            out_shape=(pltpu.VMEM(shape, BF16),) * (2 * z_size),
            scratch_shapes=[
                pltpu.VMEM((4, 2, rows, receivers), F32),
                pltpu.SemaphoreType.DMA((4,)),
            ],
            compiler_params=pltpu.CompilerParams(vmem_limit_bytes=12 << 20),
        )(kernel, place)

    def product(spectrum, parity):
        nonlocal held
        s = spectrum.reshape(n_f, 2 * n, own, rows)
        x = lax.all_to_all(s, "freq", split_axis=0, concat_axis=0, tiled=True)
        x = x.reshape(n_f, n, 2, own, rows).transpose(1, 2, 0, 3, 4).reshape(n, 2, points, rows)
        groups = gather(x)
        if held is None:
            held = hold()
        total = None
        for group in groups:
            args = [held[2 * b + h] for h in (0, 1) for b, _, _ in group]
            args += [field for _, _, field in group]
            first = total is None
            if not first:
                args.append(total)
            (total,) = call(
                functools.partial(product_body, parity, [piece[:2] for piece in group], first),
                [VMEM] * len(args),
                [sds((n, 2, points, rows), F32)],
                args,
                alias=None if first else {len(args) - 1: 0},
            )
        back = total.reshape(2 * n, n_f, own, rows).transpose(1, 0, 2, 3)
        back = lax.all_to_all(back, "freq", split_axis=0, concat_axis=0, tiled=True)
        return back.reshape(n_rows, own * rows)

    def mute(back, last, base):
        outs = [sds((own * rows, samples) if last else (n_rows, own * rows), F32)]
        args = (scale, limit, back, th, tl) + (() if base is None else (base,))
        body = functools.partial(mute_body, last, base is not None)
        return call(body, [VMEM] * len(args), outs, args)[0]

    field = start
    for iteration in range(ITERS):
        final = iteration == ITERS - 1
        back = product(field, 1.0)
        field = mute(back, False, None)
        if final:
            downgoing = mute(back, True, None)
        back = product(field, -1.0)
        field = mute(back, final, traces if final else start)
    return field.reshape(focus_start.shape), downgoing.reshape(focus_start.shape)


def solution(mesh):
    in_specs = (P(None, "freq", "rcv", None), P("freq", "rcv", None), P("freq", "rcv"), P())
    out_specs = (P("freq", "rcv", None), P("freq", "rcv", None))
    return jax.shard_map(
        functools.partial(body, mesh.shape["rcv"]),
        mesh=mesh,
        in_specs=in_specs,
        out_specs=out_specs,
        check_vma=False,
    )
```

```python
import functools
import math

import jax
import jax.numpy as jnp
from jax import lax
from jax.experimental import pallas as pl
from jax.experimental.pallas import tpu as pltpu
from jax.sharding import PartitionSpec as P


ITERS = 2
F32, BF16 = jnp.float32, jnp.bfloat16
VMEM = pl.BlockSpec(memory_space=pltpu.VMEM)
HBM = pl.BlockSpec(memory_space=pltpu.HBM)


def call(body, ins, outs, args, mib=8, alias=None, scratch=()):
    return pl.pallas_call(
        body,
        in_specs=ins,
        out_specs=tuple(VMEM for _ in outs),
        out_shape=tuple(outs),
        scratch_shapes=scratch,
        input_output_aliases=alias or {},
        compiler_params=pltpu.CompilerParams(vmem_limit_bytes=mib << 20),
    )(*args)


def halves(x):
    high = x.astype(BF16)
    return high, (x - high.astype(F32)).astype(BF16)


def dot(a, b, left, right):
    return lax.dot_general(a, b, (((left,), (right,)), ((), ())), preferred_element_type=F32)


def dot3(a, b, left, right):
    return (
        dot(a[0], b[0], left, right) + dot(a[0], b[1], left, right) + dot(a[1], b[0], left, right)
    )


def column(row, length, place):
    shape = (length, row.shape[1])
    hit = place(lax.broadcasted_iota(jnp.int32, shape, 0))
    hit = hit == lax.broadcasted_iota(jnp.int32, shape, 1)
    return jnp.sum(jnp.where(hit, row.astype(F32), 0.0), axis=1, keepdims=True)


def cosine(turn):
    x = (2.0 * math.pi) * (0.25 - jnp.minimum(turn, 1.0 - turn))
    square = x * x
    series = 0.0
    for power in range(13, 0, -2):
        series = series * square + (-1.0) ** (power // 2) / math.factorial(power)
    return series * x


def make_table(order, me, n, th, tl, scale):
    rows, samples = th.shape
    shape = (rows, samples)
    time = lax.broadcasted_iota(jnp.int32, shape, 1).astype(F32) / samples
    part = (lax.broadcasted_iota(jnp.int32, shape, 0) & 1).astype(F32) * 0.25

    def slot(r):
        return jnp.bitwise_xor(lax.div(r, 2 * n), me) * n + lax.rem(lax.div(r, 2), n)

    q = column(order, rows, slot)
    scale[...] = jnp.where(q == 0.0, 1.0, 2.0) / samples
    turn = q * time + part
    table = halves(cosine(turn - jnp.floor(turn)))
    th[...] = table[0]
    tl[...] = table[1]
    return table


def spectrum_body(n, order_in, onset_in, x_in, me, th, tl, scale, limit, *rest):
    *outs, order, onset, x, sems = rest
    pairs = ((order_in, order), (onset_in, onset), (x_in, x))
    copies = [pltpu.make_async_copy(a, b, sems.at[i]) for i, (a, b) in enumerate(pairs)]
    for copy in copies:
        copy.start()
    copies[0].wait()
    table = make_table(order[...], me[0], n, th, tl, scale)
    copies[1].wait()
    limit[...] = column(onset[...], limit.shape[0], lambda r: r).astype(jnp.int32)
    copies[2].wait()
    y = dot3(table, halves(x[...]), 1, 1)
    if len(outs) == 1:
        outs[0][...] = y
        return
    step = 2 * n
    for j in range(y.shape[0] // step):
        outs[j % 2][j // 2] = y[j * step : (j + 1) * step]


def pair_body(keep, given, limit, onset, both, *outs):
    both[0] = limit[...]
    both[1] = column(onset[...], limit.shape[0], lambda r: r).astype(jnp.int32)
    for q, out in enumerate(outs):
        out[0] = keep[q]
        out[1] = given[q]


def pair_mute_body(chips, last, base, scale, onset, th, tl, *rest):
    own, other, rest = rest[:chips], rest[chips : 2 * chips], list(rest[2 * chips :])
    base = [rest.pop(0) for _ in range(base)]
    points = 1 if last else 2
    step = own[0].shape[1]
    fields = []
    for j in range(points):
        parts = [x[i] for q in range(chips) for x, i in ((own[q], j), (other[q], 1 - j))]
        fields.append((jnp.concatenate(parts, axis=0) * scale[...]).T)
    y = dot3(halves(jnp.concatenate(fields, axis=0)), (th[...], tl[...]), 1, 0)
    t = lax.broadcasted_iota(jnp.int32, y.shape, 1)
    limit = jnp.concatenate([onset[j] for j in range(points)], axis=0)
    y = jnp.where(t < limit, y, 0.0)
    if last:
        rest[0][...] = base[0][...] + y if base else y
        return
    mine = [
        jnp.concatenate([x[2 * q * step : (2 * q + 1) * step, :] for q in range(chips)], axis=0)
        for x in (th, tl)
    ]
    z = dot3(mine, halves(y), 1, 1)
    width = z.shape[1] // 2
    for q, out in enumerate(rest):
        for j in range(2):
            piece = z[q * step : (q + 1) * step, j * width : (j + 1) * width]
            out[j] = base[q][j] + piece if base else piece


def pack_body(chips, *rest):
    pieces, outs = rest[:chips], rest[chips:]
    for q, piece in enumerate(pieces):
        outs[0][pl.ds(2 * q, 2)] = piece[...]
        for i, out in enumerate(outs[1:]):
            half = out.shape[1]
            out[pl.ds(2 * q, 2)] = piece[:, i * half : (i + 1) * half, :]


def mute_body(last, add, scale, onset, product, th, tl, *rest):
    table = (th[...], tl[...])
    y = dot3(halves((product[...] * scale[...]).T), table, 1, 0)
    t = lax.broadcasted_iota(jnp.int32, y.shape, 1)
    y = jnp.where(t < onset[...], y, 0.0)
    if not last:
        y = dot3(table, halves(y), 1, 1)
    rest[-1][...] = rest[0][...] + y if add else y


def fill(field, arrays, at):
    span, rows = field.shape[0] * 2, field.shape[3]
    for i in range(arrays[0].shape[0]):
        field[:, :, i, :] = arrays[0][i, 2 * at : 2 * at + span, :].reshape(-1, 2, rows)
    for i in range(arrays[1].shape[0]):
        field[:, :, 2 + i, :] = arrays[1][i].reshape(-1, 2, rows)


def share(x, weights):
    h, l = halves(x)
    both = jnp.concatenate([h, l], axis=0)
    rows = x.shape[0]
    out = []
    for high, low in weights:
        p = dot(both, high, 1, 0)
        out.append(p[:rows] + p[rows:] + dot(h, low, 1, 0))
    return out


def combine(parts, parity, v):
    return (
        parts[0][:v] - parity * parts[1][v:],
        parity * parts[1][:v] + parts[0][v:],
    )


def hold_body(blocks, parity, width, kernel, place, *rest):
    arrays, rest = rest[:width], rest[width:]
    outs, (total, buf, sem), scratch = rest[: 2 * blocks], rest[2 * blocks :][:3], rest[2 * blocks + 3 :]
    n, rows = kernel.shape[1:3]
    slots = buf.shape[0]

    def copy(k):
        slot = lax.rem(k, slots)
        return pltpu.make_async_copy(kernel.at[:, k], buf.at[slot], sem.at[slot])

    for k in range(min(slots - 1, n)):
        copy(k).start()
    field = arrays[0]
    if width > 1:
        field = scratch[0]
        fill(field, arrays, 0)
    v = field.shape[2]

    @pl.loop(0, n)
    def _(k):
        @pl.when(k + slots - 1 < n)
        def _():
            copy(k + slots - 1).start()

        copy(k).wait()
        slot = lax.rem(k, slots)
        weights = []
        for b in range(blocks):
            col = pl.multiple_of(jnp.bitwise_xor(place[0], b) * rows, rows)
            for c in range(2):
                x = buf[slot, c, :, pl.ds(col, rows)]
                h, l = halves(x if b == 0 else x.T)
                outs[2 * b][c, k] = h
                outs[2 * b + 1][c, k] = l
                if b == 0:
                    weights.append((h, l))
        sums = combine(share(field[k].reshape(2 * v, rows), weights), parity, v)
        for c in range(2):
            total[k, c] = sums[c]


def product_body(parity, pieces, first, chips, widths, *rest):
    count = len(pieces)
    highs, lows, rest = rest[:count], rest[count : 2 * count], list(rest[2 * count :])
    given = [[rest.pop(0) for _ in range(width)] for width in widths]
    total = None if first else rest.pop(0)
    outs = [rest.pop(0) for _ in range(max(1, chips))]
    n = (outs[0] if first else total).shape[0]
    fields = []
    for (_, at), arrays in zip(pieces, given):
        if len(arrays) == 1:
            fields.append(arrays[0])
            continue
        fields.append(rest.pop(0))
        fill(fields[-1], arrays, at)
    v, rows = fields[0].shape[2:]
    cuts = {0, n} | {at for _, at in pieces}
    cuts = sorted(cuts | {at + x.shape[0] for (_, at), x in zip(pieces, fields)})

    def one(k, here):
        parts = None
        for high, low, at, x in here:
            weights = [(high[c, k], low[c, k]) for c in range(2)]
            p = share(x[k - at].reshape(2 * v, rows), weights)
            parts = p if parts is None else [i + j for i, j in zip(parts, p)]
        sums = [None, None] if parts is None else list(combine(parts, parity, v))
        for c in range(2):
            if not first:
                sums[c] = total[k, c] if sums[c] is None else total[k, c] + sums[c]
            if not chips:
                outs[0][k, c] = sums[c]
                continue
            for i in range(v):
                outs[i // 2][i % 2, pl.ds(2 * k + c, 1), :] = sums[c][i : i + 1]

    for begin, end in zip(cuts[:-1], cuts[1:]):
        here = [
            (high, low, at, x)
            for (_, at), high, low, x in zip(pieces, highs, lows, fields)
            if at <= begin and end <= at + x.shape[0]
        ]
        if not here and not chips:
            continue
        step = math.gcd(end - begin, max(1, 8 // max(1, len(here))))

        @pl.loop(begin // step, end // step)
        def _(i):
            for j in range(step):
                one(i * step + j, here)


def body(z_size, kernel, focus_start, onset, freq_order):
    sds = jax.ShapeDtypeStruct
    _, n, rows, receivers = kernel.shape
    own, samples = focus_start.shape[0], focus_start.shape[2]
    n_f = freq_order.shape[0] // n
    points = n_f * own
    chips = 4 if n_f == 8 and own == 1 and n % 2 == 0 and z_size == 4 else 0
    place = lax.axis_index("rcv")[None].astype(jnp.int32)
    me = lax.axis_index("freq")[None].astype(jnp.int32) * (1 if chips else 0)
    smem = pl.BlockSpec(memory_space=pltpu.SMEM)

    n_rows = 2 * freq_order.shape[0]
    traces = focus_start.reshape(own * rows, samples)
    if chips:
        spectra = [sds((chips, 2 * n, rows), F32)] * 2
    else:
        spectra = [sds((n_rows, own * rows), F32)]
    th, tl, scale, limit, *start = call(
        functools.partial(spectrum_body, n),
        [HBM] * 3 + [smem],
        [sds((n_rows, samples), BF16)] * 2
        + [sds((n_rows, 1), F32), sds((own * rows, 1), jnp.int32)]
        + spectra,
        [
            pltpu.with_memory_space_constraint(x, pltpu.HBM)
            for x in (freq_order.reshape(1, -1), onset.reshape(1, -1), traces)
        ]
        + [me],
        scratch=[
            pltpu.VMEM((1, n_rows // 2), jnp.int32),
            pltpu.VMEM((1, own * rows), jnp.int32),
            pltpu.VMEM((own * rows, samples), F32),
            pltpu.SemaphoreType.DMA((3,)),
        ],
    )

    def trade(x, d):
        return lax.ppermute(x, "freq", [(i, i ^ d) for i in range(n_f)])

    def across(pieces):
        moved = {q: trade(pieces[q], 2 * q) for q in (3, 1, 2)}
        return [pieces[0]] + [moved[q] for q in (1, 2, 3)]

    if chips:
        given = trade(start[1], 1)
        limit, *start = call(
            pair_body,
            [VMEM] * 4,
            [sds((2, rows, 1), jnp.int32)] + [sds((2, 2 * n, rows), F32)] * chips,
            (start[0], given, limit, trade(onset, 1)),
        )
    else:
        start = start[0]

    held = None

    def shift(x, d):
        return lax.ppermute(x, "rcv", [(i, i ^ d) for i in range(z_size)])

    def gather(near, x, low=None, high=None):
        if z_size != 4 or n % 2 or held is None:
            far = {d: shift(x, d) for d in range(1, z_size)}
            pieces = [(0, 0, x)] + [(d, 0, far[d]) for d in far]
        else:
            half = n // 2
            b0 = shift(low, 2)
            a = shift(x, 1)
            c1 = shift(high, 3)
            b1 = shift(high, 2)
            c0 = shift(b0, 1)
            pieces = [(0, 0, x), (2, 0, b0), (1, 0, a), (3, half, c1), (3, 0, c0), (2, half, b1)]
        return [
            [(b, at, [near[b], array] if near else [array])] for b, at, array in pieces
        ]

    def field_scratch(arrays):
        if len(arrays) == 1:
            return []
        return [pltpu.VMEM((arrays[1].shape[1] // 2, 2, points, rows), F32)]

    def hold(arrays, parity):
        shape = (2, n, rows, rows)
        *outs, total = pl.pallas_call(
            functools.partial(hold_body, z_size, parity, len(arrays)),
            in_specs=[HBM, smem] + [VMEM] * len(arrays),
            out_specs=(VMEM,) * (2 * z_size + 1),
            out_shape=(pltpu.VMEM(shape, BF16),) * (2 * z_size)
            + (sds((n, 2, points, rows), F32),),
            scratch_shapes=[pltpu.VMEM((4, 2, rows, receivers), F32), pltpu.SemaphoreType.DMA((4,))]
            + field_scratch(arrays),
            compiler_params=pltpu.CompilerParams(vmem_limit_bytes=12 << 20),
        )(kernel, place, *arrays)
        return outs, [total]

    def product(spectrum, parity):
        nonlocal held
        if chips:
            pieces = across(spectrum)
            near = [pieces[0]] + [shift(pieces[0], d) for d in range(1, z_size)]
            far = points - 2
            shapes = [(far, 2 * n, rows)] + ([(far, n, rows)] * 2 if held else [])
            packed = call(
                functools.partial(pack_body, chips - 1),
                [VMEM] * (chips - 1),
                [sds(shape, F32) for shape in shapes],
                pieces[1:],
            )
            groups = gather(near, *packed)
        else:
            s = spectrum.reshape(n_f, 2 * n, own, rows)
            x = lax.all_to_all(s, "freq", split_axis=0, concat_axis=0, tiled=True)
            x = x.reshape(n_f, n, 2, own, rows).transpose(1, 2, 0, 3, 4)
            x = x.reshape(n, 2, points, rows)
            groups = gather(None, x, x[: n // 2], x[n // 2 :])
        total = None
        if held is None:
            held, total = hold(groups.pop(0)[0][2], parity)
        for step, group in enumerate(groups):
            args = [held[2 * b + h] for h in (0, 1) for b, _, _ in group]
            widths = [len(arrays) for _, _, arrays in group]
            args += [x for _, _, arrays in group for x in arrays]
            scratch = [x for _, _, arrays in group for x in field_scratch(arrays)]
            first, end = total is None, chips if step == len(groups) - 1 else 0
            outs = [sds((2, 2 * n, rows), F32)] * end or [sds((n, 2, points, rows), F32)]
            if not first:
                args += total
            pieces = [piece[:2] for piece in group]
            total = call(
                functools.partial(product_body, parity, pieces, first, end, widths),
                [VMEM] * len(args),
                outs,
                args,
                scratch=scratch,
                alias=None if first or end else {len(args) - 1: 0},
            )
        if chips:
            back = across(total)
            return back + [trade(x, 1) for x in back]
        back = total[0].reshape(2 * n, n_f, own, rows).transpose(1, 0, 2, 3)
        back = lax.all_to_all(back, "freq", split_axis=0, concat_axis=0, tiled=True)
        return back.reshape(n_rows, own * rows)

    def mute(back, last, base):
        if chips:
            base = [] if base is None else [base] if last else base
            outs = [sds((rows, samples), F32)] if last else [sds((2, 2 * n, rows), F32)] * chips
            args = (scale, limit, th, tl, *back, *base)
            body = functools.partial(pair_mute_body, chips, last, len(base))
            got = call(body, [VMEM] * len(args), outs, args)
            return got[0] if last else got
        outs = [sds((own * rows, samples) if last else (n_rows, own * rows), F32)]
        args = (scale, limit, back, th, tl) + (() if base is None else (base,))
        body = functools.partial(mute_body, last, base is not None)
        return call(body, [VMEM] * len(args), outs, args)[0]

    field = start
    for iteration in range(ITERS):
        final = iteration == ITERS - 1
        back = product(field, 1.0)
        field = mute(back, False, None)
        if final:
            downgoing = mute(back, True, None)
        back = product(field, -1.0)
        field = mute(back, final, traces if final else start)
    return field.reshape(focus_start.shape), downgoing.reshape(focus_start.shape)


def solution(mesh):
    in_specs = (P(None, "freq", "rcv", None), P("freq", "rcv", None), P("freq", "rcv"), P())
    out_specs = (P("freq", "rcv", None), P("freq", "rcv", None))
    return jax.shard_map(
        functools.partial(body, mesh.shape["rcv"]),
        mesh=mesh,
        in_specs=in_specs,
        out_specs=out_specs,
        check_vma=False,
    )
```

```python
import functools
import math

import jax
import jax.numpy as jnp
from jax import lax
from jax.experimental import pallas as pl
from jax.experimental.pallas import tpu as pltpu
from jax.sharding import PartitionSpec as P


ITERS = 2
F32, BF16 = jnp.float32, jnp.bfloat16
VMEM = pl.BlockSpec(memory_space=pltpu.VMEM)
HBM = pl.BlockSpec(memory_space=pltpu.HBM)


def call(body, ins, outs, args, mib=8, alias=None, scratch=()):
    return pl.pallas_call(
        body,
        in_specs=ins,
        out_specs=tuple(VMEM for _ in outs),
        out_shape=tuple(outs),
        scratch_shapes=scratch,
        input_output_aliases=alias or {},
        compiler_params=pltpu.CompilerParams(vmem_limit_bytes=mib << 20),
    )(*args)


def halves(x):
    high = x.astype(BF16)
    return high, (x - high.astype(F32)).astype(BF16)


def dot(a, b, left, right):
    return lax.dot_general(a, b, (((left,), (right,)), ((), ())), preferred_element_type=F32)


def dot3(a, b, left, right):
    return (
        dot(a[0], b[0], left, right) + dot(a[0], b[1], left, right) + dot(a[1], b[0], left, right)
    )


def column(row, length, place):
    shape = (length, row.shape[1])
    hit = place(lax.broadcasted_iota(jnp.int32, shape, 0))
    hit = hit == lax.broadcasted_iota(jnp.int32, shape, 1)
    return jnp.sum(jnp.where(hit, row.astype(F32), 0.0), axis=1, keepdims=True)


def cosine(turn):
    x = (2.0 * math.pi) * (0.25 - jnp.minimum(turn, 1.0 - turn))
    square = x * x
    series = 0.0
    for power in range(13, 0, -2):
        series = series * square + (-1.0) ** (power // 2) / math.factorial(power)
    return series * x


def make_table(order, me, n, samples, scale):
    rows = scale.shape[0]
    shape = (rows, samples)
    time = lax.broadcasted_iota(jnp.int32, shape, 1).astype(F32) / samples
    part = (lax.broadcasted_iota(jnp.int32, shape, 0) & 1).astype(F32) * 0.25

    def slot(r):
        return jnp.bitwise_xor(lax.div(r, 2 * n), me) * n + lax.rem(lax.div(r, 2), n)

    q = column(order, rows, slot)
    scale[...] = jnp.where(q == 0.0, 1.0, 2.0) / samples
    turn = q * time + part
    return cosine(turn - jnp.floor(turn))


def spectrum_body(n, order_in, onset_in, x_in, th, tl, scale, limit, out, order, onset, x, sems):
    pairs = ((order_in, order), (onset_in, onset), (x_in, x))
    copies = [pltpu.make_async_copy(a, b, sems.at[i]) for i, (a, b) in enumerate(pairs)]
    for copy in copies:
        copy.start()
    copies[0].wait()
    table = halves(make_table(order[...], 0, n, x.shape[1], scale))
    th[...] = table[0]
    tl[...] = table[1]
    copies[1].wait()
    limit[...] = column(onset[...], limit.shape[0], lambda r: r).astype(jnp.int32)
    copies[2].wait()
    out[...] = dot3(table, halves(x[...]), 1, 1)


def pair_table_body(chips, n, order_in, onset_in, x_in, me, mh, ml, bh, bl, scale, *rest):
    onset, x, order, sems = rest
    pairs = ((order_in, order), (onset_in, onset), (x_in, x))
    copies = [pltpu.make_async_copy(a, b, sems.at[i]) for i, (a, b) in enumerate(pairs)]
    for copy in copies:
        copy.start()
    copies[0].wait()
    table = make_table(order[...], me[0], n, x.shape[1], scale)
    step = 2 * n
    mine = [table[2 * q * step : (2 * q + 1) * step] for q in range(chips)]
    mh[...], ml[...] = halves(jnp.concatenate(mine, axis=0))
    bh[...], bl[...] = halves(table.T)
    copies[1].wait()
    copies[2].wait()


def pair_spectrum_body(mh, ml, own, other, onset, other_onset, limit, *outs):
    step, width = outs[0].shape[1:]
    y = jnp.concatenate([own[...], other[...]], axis=0)
    z = dot3((mh[...], ml[...]), halves(y), 1, 1)
    for q, out in enumerate(outs):
        for j in range(2):
            out[j] = z[q * step : (q + 1) * step, j * width : (j + 1) * width]
    limit[...] = jnp.concatenate([onset[...], other_onset[...]], axis=1)


def pair_mute_body(chips, last, base, scale, onset, mh, ml, bh, bl, *rest):
    own, other, rest = rest[:chips], rest[chips : 2 * chips], list(rest[2 * chips :])
    base = [rest.pop(0) for _ in range(base)]
    step, width = own[0].shape[1:]
    fields = []
    for j in range(1 if last else 2):
        parts = [x[i] for q in range(chips) for x, i in ((own[q], j), (other[q], 1 - j))]
        fields.append(jnp.concatenate(parts, axis=0))
    fields = jnp.concatenate(fields, axis=1) * scale[...]
    y = dot3((bh[...], bl[...]), halves(fields), 1, 0)
    t = lax.broadcasted_iota(jnp.int32, y.shape, 0)
    y = jnp.where(t < onset[:, : y.shape[1]], y, 0.0)
    if last:
        rest[0][...] = base[0][...] + y.T if base else y.T
        return
    z = dot3((mh[...], ml[...]), halves(y), 1, 0)
    for q, out in enumerate(rest):
        for j in range(2):
            piece = z[q * step : (q + 1) * step, j * width : (j + 1) * width]
            out[j] = base[q][j] + piece if base else piece


def pack_body(chips, *rest):
    pieces, outs = rest[:chips], rest[chips:]
    for q, piece in enumerate(pieces):
        outs[0][pl.ds(2 * q, 2)] = piece[...]
        for i, out in enumerate(outs[1:]):
            half = out.shape[1]
            out[pl.ds(2 * q, 2)] = piece[:, i * half : (i + 1) * half, :]


def mute_body(last, add, scale, onset, product, th, tl, *rest):
    table = (th[...], tl[...])
    y = dot3(halves((product[...] * scale[...]).T), table, 1, 0)
    t = lax.broadcasted_iota(jnp.int32, y.shape, 1)
    y = jnp.where(t < onset[...], y, 0.0)
    if not last:
        y = dot3(table, halves(y), 1, 1)
    rest[-1][...] = rest[0][...] + y if add else y


def fill(field, arrays, at):
    span, rows = field.shape[0] * 2, field.shape[3]
    for i in range(arrays[0].shape[0]):
        field[:, :, i, :] = arrays[0][i, 2 * at : 2 * at + span, :].reshape(-1, 2, rows)
    for i in range(arrays[1].shape[0]):
        field[:, :, 2 + i, :] = arrays[1][i].reshape(-1, 2, rows)


def share(x, weights):
    h, l = halves(x)
    both = jnp.concatenate([h, l], axis=0)
    rows = x.shape[0]
    out = []
    for high, low in weights:
        p = dot(both, high, 1, 0)
        out.append(p[:rows] + p[rows:] + dot(h, low, 1, 0))
    return out


def combine(parts, parity, v):
    return (
        parts[0][:v] - parity * parts[1][v:],
        parity * parts[1][:v] + parts[0][v:],
    )


def hold_body(blocks, parity, width, kernel, place, *rest):
    arrays, rest = rest[:width], rest[width:]
    outs, (total, buf, sem), scratch = rest[: 2 * blocks], rest[2 * blocks :][:3], rest[2 * blocks + 3 :]
    n, rows = kernel.shape[1:3]
    slots = buf.shape[0]

    def copy(k):
        slot = lax.rem(k, slots)
        return pltpu.make_async_copy(kernel.at[:, k], buf.at[slot], sem.at[slot])

    for k in range(min(slots - 1, n)):
        copy(k).start()
    field = arrays[0]
    if width > 1:
        field = scratch[0]
        fill(field, arrays, 0)
    v = field.shape[2]

    @pl.loop(0, n)
    def _(k):
        @pl.when(k + slots - 1 < n)
        def _():
            copy(k + slots - 1).start()

        copy(k).wait()
        slot = lax.rem(k, slots)
        weights = []
        for b in range(blocks):
            col = pl.multiple_of(jnp.bitwise_xor(place[0], b) * rows, rows)
            for c in range(2):
                x = buf[slot, c, :, pl.ds(col, rows)]
                h, l = halves(x if b == 0 else x.T)
                outs[2 * b][c, k] = h
                outs[2 * b + 1][c, k] = l
                if b == 0:
                    weights.append((h, l))
        sums = combine(share(field[k].reshape(2 * v, rows), weights), parity, v)
        for c in range(2):
            total[k, c] = sums[c]


def product_body(parity, pieces, first, chips, widths, *rest):
    count = len(pieces)
    highs, lows, rest = rest[:count], rest[count : 2 * count], list(rest[2 * count :])
    given = [[rest.pop(0) for _ in range(width)] for width in widths]
    total = None if first else rest.pop(0)
    outs = [rest.pop(0) for _ in range(max(1, chips))]
    n = (outs[0] if first else total).shape[0]
    fields = []
    for (_, at), arrays in zip(pieces, given):
        if len(arrays) == 1:
            fields.append(arrays[0])
            continue
        fields.append(rest.pop(0))
        fill(fields[-1], arrays, at)
    v, rows = fields[0].shape[2:]
    cuts = {0, n} | {at for _, at in pieces}
    cuts = sorted(cuts | {at + x.shape[0] for (_, at), x in zip(pieces, fields)})

    def one(k, here):
        parts = None
        for high, low, at, x in here:
            weights = [(high[c, k], low[c, k]) for c in range(2)]
            p = share(x[k - at].reshape(2 * v, rows), weights)
            parts = p if parts is None else [i + j for i, j in zip(parts, p)]
        sums = [None, None] if parts is None else list(combine(parts, parity, v))
        for c in range(2):
            if not first:
                sums[c] = total[k, c] if sums[c] is None else total[k, c] + sums[c]
            if not chips:
                outs[0][k, c] = sums[c]
                continue
            for i in range(v):
                outs[i // 2][i % 2, pl.ds(2 * k + c, 1), :] = sums[c][i : i + 1]

    for begin, end in zip(cuts[:-1], cuts[1:]):
        here = [
            (high, low, at, x)
            for (_, at), high, low, x in zip(pieces, highs, lows, fields)
            if at <= begin and end <= at + x.shape[0]
        ]
        if not here and not chips:
            continue
        step = math.gcd(end - begin, max(1, 8 // max(1, len(here))))

        @pl.loop(begin // step, end // step)
        def _(i):
            for j in range(step):
                one(i * step + j, here)


def body(z_size, kernel, focus_start, onset, freq_order):
    sds = jax.ShapeDtypeStruct
    _, n, rows, receivers = kernel.shape
    own, samples = focus_start.shape[0], focus_start.shape[2]
    n_f = freq_order.shape[0] // n
    points = n_f * own
    chips = 4 if n_f == 8 and own == 1 and n % 2 == 0 and z_size == 4 else 0
    place = lax.axis_index("rcv")[None].astype(jnp.int32)
    me = lax.axis_index("freq")[None].astype(jnp.int32)
    smem = pl.BlockSpec(memory_space=pltpu.SMEM)

    n_rows = 2 * freq_order.shape[0]
    traces = focus_start.reshape(own * rows, samples)

    def trade(x, d):
        return lax.ppermute(x, "freq", [(i, i ^ d) for i in range(n_f)])

    def across(pieces):
        moved = {q: trade(pieces[q], 2 * q) for q in (3, 1, 2)}
        return [pieces[0]] + [moved[q] for q in (1, 2, 3)]

    def from_hbm(*arrays):
        return [pltpu.with_memory_space_constraint(x, pltpu.HBM) for x in arrays]

    order, limit = freq_order.reshape(1, -1), onset.reshape(1, -1)
    order_scratch = pltpu.VMEM((1, n_rows // 2), jnp.int32)
    if chips:
        given = trade(traces, 1)
        other = trade(limit, 1)
        *table, scale, near_limit, local = call(
            functools.partial(pair_table_body, chips, n),
            [HBM] * 3 + [smem],
            [sds((n_rows // 2, samples), BF16)] * 2
            + [sds((samples, n_rows), BF16)] * 2
            + [sds((n_rows, 1), F32), sds((1, rows), jnp.int32), sds((rows, samples), F32)],
            [*from_hbm(order, limit, traces), me],
            scratch=[order_scratch, pltpu.SemaphoreType.DMA((3,))],
        )
        limit, *start = call(
            pair_spectrum_body,
            [VMEM] * 6,
            [sds((1, 2 * rows), jnp.int32)] + [sds((2, 2 * n, rows), F32)] * chips,
            (*table[:2], local, given, near_limit, other),
        )
    else:
        *table, scale, limit, start = call(
            functools.partial(spectrum_body, n),
            [HBM] * 3,
            [sds((n_rows, samples), BF16)] * 2
            + [sds((n_rows, 1), F32), sds((own * rows, 1), jnp.int32)]
            + [sds((n_rows, own * rows), F32)],
            from_hbm(order, limit, traces),
            scratch=[
                order_scratch,
                pltpu.VMEM((1, own * rows), jnp.int32),
                pltpu.VMEM((own * rows, samples), F32),
                pltpu.SemaphoreType.DMA((3,)),
            ],
        )

    held = None

    def shift(x, d):
        return lax.ppermute(x, "rcv", [(i, i ^ d) for i in range(z_size)])

    def gather(near, x, low=None, high=None):
        if z_size != 4 or n % 2 or held is None:
            far = {d: shift(x, d) for d in range(1, z_size)}
            pieces = [(0, 0, x)] + [(d, 0, far[d]) for d in far]
        else:
            half = n // 2
            b0 = shift(low, 2)
            a = shift(x, 1)
            c1 = shift(high, 3)
            b1 = shift(high, 2)
            c0 = shift(b0, 1)
            pieces = [(0, 0, x), (2, 0, b0), (1, 0, a), (3, half, c1), (3, 0, c0), (2, half, b1)]
        return [
            [(b, at, [near[b], array] if near else [array])] for b, at, array in pieces
        ]

    def field_scratch(arrays):
        if len(arrays) == 1:
            return []
        return [pltpu.VMEM((arrays[1].shape[1] // 2, 2, points, rows), F32)]

    def hold(arrays, parity):
        shape = (2, n, rows, rows)
        *outs, total = pl.pallas_call(
            functools.partial(hold_body, z_size, parity, len(arrays)),
            in_specs=[HBM, smem] + [VMEM] * len(arrays),
            out_specs=(VMEM,) * (2 * z_size + 1),
            out_shape=(pltpu.VMEM(shape, BF16),) * (2 * z_size)
            + (sds((n, 2, points, rows), F32),),
            scratch_shapes=[pltpu.VMEM((4, 2, rows, receivers), F32), pltpu.SemaphoreType.DMA((4,))]
            + field_scratch(arrays),
            compiler_params=pltpu.CompilerParams(vmem_limit_bytes=12 << 20),
        )(kernel, place, *arrays)
        return outs, [total]

    def product(spectrum, parity):
        nonlocal held
        if chips:
            pieces = across(spectrum)
            near = [pieces[0]] + [shift(pieces[0], d) for d in range(1, z_size)]
            far = points - 2
            shapes = [(far, 2 * n, rows)] + ([(far, n, rows)] * 2 if held else [])
            packed = call(
                functools.partial(pack_body, chips - 1),
                [VMEM] * (chips - 1),
                [sds(shape, F32) for shape in shapes],
                pieces[1:],
            )
            groups = gather(near, *packed)
        else:
            s = spectrum.reshape(n_f, 2 * n, own, rows)
            x = lax.all_to_all(s, "freq", split_axis=0, concat_axis=0, tiled=True)
            x = x.reshape(n_f, n, 2, own, rows).transpose(1, 2, 0, 3, 4)
            x = x.reshape(n, 2, points, rows)
            groups = gather(None, x, x[: n // 2], x[n // 2 :])
        total = None
        if held is None:
            held, total = hold(groups.pop(0)[0][2], parity)
        for step, group in enumerate(groups):
            args = [held[2 * b + h] for h in (0, 1) for b, _, _ in group]
            widths = [len(arrays) for _, _, arrays in group]
            args += [x for _, _, arrays in group for x in arrays]
            scratch = [x for _, _, arrays in group for x in field_scratch(arrays)]
            first, end = total is None, chips if step == len(groups) - 1 else 0
            outs = [sds((2, 2 * n, rows), F32)] * end or [sds((n, 2, points, rows), F32)]
            if not first:
                args += total
            pieces = [piece[:2] for piece in group]
            total = call(
                functools.partial(product_body, parity, pieces, first, end, widths),
                [VMEM] * len(args),
                outs,
                args,
                scratch=scratch,
                alias=None if first or end else {len(args) - 1: 0},
            )
        if chips:
            back = across(total)
            return back + [trade(x, 1) for x in back]
        back = total[0].reshape(2 * n, n_f, own, rows).transpose(1, 0, 2, 3)
        back = lax.all_to_all(back, "freq", split_axis=0, concat_axis=0, tiled=True)
        return back.reshape(n_rows, own * rows)

    def mute(back, last, base):
        if chips:
            base = [] if base is None else [base] if last else base
            outs = [sds((rows, samples), F32)] if last else [sds((2, 2 * n, rows), F32)] * chips
            args = (scale, limit, *table, *back, *base)
            body = functools.partial(pair_mute_body, chips, last, len(base))
            got = call(body, [VMEM] * len(args), outs, args)
            return got[0] if last else got
        outs = [sds((own * rows, samples) if last else (n_rows, own * rows), F32)]
        args = (scale, limit, back, *table) + (() if base is None else (base,))
        body = functools.partial(mute_body, last, base is not None)
        return call(body, [VMEM] * len(args), outs, args)[0]

    field = start
    for iteration in range(ITERS):
        final = iteration == ITERS - 1
        back = product(field, 1.0)
        field = mute(back, False, None)
        if final:
            downgoing = mute(back, True, None)
        back = product(field, -1.0)
        field = mute(back, final, traces if final else start)
    return field.reshape(focus_start.shape), downgoing.reshape(focus_start.shape)


def solution(mesh):
    in_specs = (P(None, "freq", "rcv", None), P("freq", "rcv", None), P("freq", "rcv"), P())
    out_specs = (P("freq", "rcv", None), P("freq", "rcv", None))
    return jax.shard_map(
        functools.partial(body, mesh.shape["rcv"]),
        mesh=mesh,
        in_specs=in_specs,
        out_specs=out_specs,
        check_vma=False,
    )
```

```python
import functools
import math

import jax
import jax.numpy as jnp
from jax import lax
from jax.experimental import pallas as pl
from jax.experimental.pallas import tpu as pltpu
from jax.sharding import PartitionSpec as P


ITERS = 2
F32, BF16 = jnp.float32, jnp.bfloat16
VMEM = pl.BlockSpec(memory_space=pltpu.VMEM)
HBM = pl.BlockSpec(memory_space=pltpu.HBM)


def call(body, ins, outs, args, mib=8, alias=None, scratch=()):
    return pl.pallas_call(
        body,
        in_specs=ins,
        out_specs=tuple(VMEM for _ in outs),
        out_shape=tuple(outs),
        scratch_shapes=scratch,
        input_output_aliases=alias or {},
        compiler_params=pltpu.CompilerParams(vmem_limit_bytes=mib << 20),
    )(*args)


def halves(x):
    high = x.astype(BF16)
    return high, (x - high.astype(F32)).astype(BF16)


def dot(a, b, left, right):
    return lax.dot_general(a, b, (((left,), (right,)), ((), ())), preferred_element_type=F32)


def dot3(a, b, left, right):
    return (
        dot(a[0], b[0], left, right) + dot(a[0], b[1], left, right) + dot(a[1], b[0], left, right)
    )


def column(row, length, place):
    shape = (length, row.shape[1])
    hit = place(lax.broadcasted_iota(jnp.int32, shape, 0))
    hit = hit == lax.broadcasted_iota(jnp.int32, shape, 1)
    return jnp.sum(jnp.where(hit, row.astype(F32), 0.0), axis=1, keepdims=True)


def cosine(turn):
    x = (2.0 * math.pi) * (0.25 - jnp.minimum(turn, 1.0 - turn))
    square = x * x
    series = 0.0
    for power in range(13, 0, -2):
        series = series * square + (-1.0) ** (power // 2) / math.factorial(power)
    return series * x


def make_table(order, me, n, samples, scale):
    rows = scale.shape[0]
    shape = (rows, samples)
    time = lax.broadcasted_iota(jnp.int32, shape, 1).astype(F32) / samples
    part = (lax.broadcasted_iota(jnp.int32, shape, 0) & 1).astype(F32) * 0.25

    def slot(r):
        return jnp.bitwise_xor(lax.div(r, 2 * n), me) * n + lax.rem(lax.div(r, 2), n)

    q = column(order, rows, slot)
    scale[...] = jnp.where(q == 0.0, 1.0, 2.0) / samples
    turn = q * time + part
    return cosine(turn - jnp.floor(turn))


def spectrum_body(n, order_in, onset_in, x_in, th, tl, scale, limit, out, order, onset, x, sems):
    pairs = ((order_in, order), (onset_in, onset), (x_in, x))
    copies = [pltpu.make_async_copy(a, b, sems.at[i]) for i, (a, b) in enumerate(pairs)]
    for copy in copies:
        copy.start()
    copies[0].wait()
    table = halves(make_table(order[...], 0, n, x.shape[1], scale))
    th[...] = table[0]
    tl[...] = table[1]
    copies[1].wait()
    limit[...] = column(onset[...], limit.shape[0], lambda r: r).astype(jnp.int32)
    copies[2].wait()
    out[...] = dot3(table, halves(x[...]), 1, 1)


def pair_table_body(chips, n, order_in, onset_in, x_in, me, mh, ml, bh, bl, scale, *rest):
    onset, x, order, sems = rest
    pairs = ((order_in, order), (onset_in, onset), (x_in, x))
    copies = [pltpu.make_async_copy(a, b, sems.at[i]) for i, (a, b) in enumerate(pairs)]
    for copy in copies:
        copy.start()
    copies[0].wait()
    table = make_table(order[...], me[0], n, x.shape[1], scale)
    step = 2 * n
    mine = [table[2 * q * step : (2 * q + 1) * step] for q in range(chips)]
    mh[...], ml[...] = halves(jnp.concatenate(mine, axis=0))
    bh[...], bl[...] = halves(table.T)
    copies[1].wait()
    copies[2].wait()


def pair_spectrum_body(mh, ml, own, other, onset, other_onset, limit, *outs):
    step, width = outs[0].shape[1:]
    y = jnp.concatenate([own[...], other[...]], axis=0)
    z = dot3((mh[...], ml[...]), halves(y), 1, 1)
    for q, out in enumerate(outs):
        for j in range(2):
            out[j] = z[q * step : (q + 1) * step, j * width : (j + 1) * width]
    limit[...] = jnp.concatenate([onset[...], other_onset[...]], axis=1)


def pair_mute_body(chips, last, base, scale, onset, mh, ml, bh, bl, *rest):
    own, other, rest = rest[:chips], rest[chips : 2 * chips], list(rest[2 * chips :])
    base = [rest.pop(0) for _ in range(base)]
    step, width = own[0].shape[1:]
    fields = []
    for j in range(1 if last else 2):
        parts = [x[i] for q in range(chips) for x, i in ((own[q], j), (other[q], 1 - j))]
        fields.append(jnp.concatenate(parts, axis=0))
    fields = jnp.concatenate(fields, axis=1) * scale[...]
    y = dot3((bh[...], bl[...]), halves(fields), 1, 0)
    t = lax.broadcasted_iota(jnp.int32, y.shape, 0)
    y = jnp.where(t < onset[:, : y.shape[1]], y, 0.0)
    if last:
        rest[0][...] = base[0][...] + y.T if base else y.T
        return
    z = dot3((mh[...], ml[...]), halves(y), 1, 0)
    for q, out in enumerate(rest):
        for j in range(2):
            piece = z[q * step : (q + 1) * step, j * width : (j + 1) * width]
            out[j] = base[q][j] + piece if base else piece


def pack_body(chips, *rest):
    pieces, outs = rest[:chips], rest[chips:]
    for q, piece in enumerate(pieces):
        outs[0][pl.ds(2 * q, 2)] = piece[...]
        for i, out in enumerate(outs[1:]):
            half = out.shape[1]
            out[pl.ds(2 * q, 2)] = piece[:, i * half : (i + 1) * half, :]


def mute_body(last, add, scale, onset, product, th, tl, *rest):
    table = (th[...], tl[...])
    y = dot3(halves((product[...] * scale[...]).T), table, 1, 0)
    t = lax.broadcasted_iota(jnp.int32, y.shape, 1)
    y = jnp.where(t < onset[...], y, 0.0)
    if not last:
        y = dot3(table, halves(y), 1, 1)
    rest[-1][...] = rest[0][...] + y if add else y


def fill(field, arrays, at):
    span, rows = field.shape[0] * 2, field.shape[3]
    for i in range(arrays[0].shape[0]):
        field[:, :, i, :] = arrays[0][i, 2 * at : 2 * at + span, :].reshape(-1, 2, rows)
    for i in range(arrays[1].shape[0]):
        field[:, :, 2 + i, :] = arrays[1][i].reshape(-1, 2, rows)


def share(x, weights):
    h, l = halves(x)
    both = jnp.concatenate([h, l], axis=0)
    rows = x.shape[0]
    out = []
    for high, low in weights:
        p = dot(both, high, 1, 0)
        out.append(p[:rows] + p[rows:] + dot(h, low, 1, 0))
    return out


def combine(parts, parity, v):
    return (
        parts[0][:v] - parity * parts[1][v:],
        parity * parts[1][:v] + parts[0][v:],
    )


def hold_body(blocks, parity, width, kernel, place, *rest):
    arrays, rest = rest[:width], rest[width:]
    outs, (total, buf, sem), scratch = rest[: 2 * blocks], rest[2 * blocks :][:3], rest[2 * blocks + 3 :]
    n, rows = kernel.shape[1:3]
    slots = buf.shape[0]

    def copy(k):
        slot = lax.rem(k, slots)
        return pltpu.make_async_copy(kernel.at[:, k], buf.at[slot], sem.at[slot])

    for k in range(min(slots - 1, n)):
        copy(k).start()
    field = arrays[0]
    if width > 1:
        field = scratch[0]
        fill(field, arrays, 0)
    v = field.shape[2]

    @pl.loop(0, n)
    def _(k):
        @pl.when(k + slots - 1 < n)
        def _():
            copy(k + slots - 1).start()

        copy(k).wait()
        slot = lax.rem(k, slots)
        weights = []
        for b in range(blocks):
            col = pl.multiple_of(jnp.bitwise_xor(place[0], b) * rows, rows)
            for c in range(2):
                x = buf[slot, c, :, pl.ds(col, rows)]
                h, l = halves(x if b == 0 else x.T)
                outs[2 * b][c, k] = h
                outs[2 * b + 1][c, k] = l
                if b == 0:
                    weights.append((h, l))
        sums = combine(share(field[k].reshape(2 * v, rows), weights), parity, v)
        for c in range(2):
            total[k, c] = sums[c]


def product_body(parity, pieces, first, chips, widths, *rest):
    count = len(pieces)
    highs, lows, rest = rest[:count], rest[count : 2 * count], list(rest[2 * count :])
    given = [[rest.pop(0) for _ in range(width)] for width in widths]
    total = None if first else rest.pop(0)
    outs = [rest.pop(0) for _ in range(max(1, chips))]
    n = (outs[0] if first else total).shape[0]
    fields = []
    for (_, at), arrays in zip(pieces, given):
        if len(arrays) == 1:
            fields.append(arrays[0])
            continue
        fields.append(rest.pop(0))
        fill(fields[-1], arrays, at)
    v, rows = fields[0].shape[2:]
    cuts = {0, n} | {at for _, at in pieces}
    cuts = sorted(cuts | {at + x.shape[0] for (_, at), x in zip(pieces, fields)})

    def one(k, here):
        parts = None
        for high, low, at, x in here:
            weights = [(high[c, k], low[c, k]) for c in range(2)]
            p = share(x[k - at].reshape(2 * v, rows), weights)
            parts = p if parts is None else [i + j for i, j in zip(parts, p)]
        sums = [None, None] if parts is None else list(combine(parts, parity, v))
        for c in range(2):
            if not first:
                sums[c] = total[k, c] if sums[c] is None else total[k, c] + sums[c]
            if not chips:
                outs[0][k, c] = sums[c]
                continue
            for i in range(v):
                outs[i // 2][i % 2, pl.ds(2 * k + c, 1), :] = sums[c][i : i + 1]

    for begin, end in zip(cuts[:-1], cuts[1:]):
        here = [
            (high, low, at, x)
            for (_, at), high, low, x in zip(pieces, highs, lows, fields)
            if at <= begin and end <= at + x.shape[0]
        ]
        if not here and not chips:
            continue
        step = math.gcd(end - begin, max(1, 16 // max(1, len(here))))

        @pl.loop(begin // step, end // step)
        def _(i):
            for j in range(step):
                one(i * step + j, here)


def body(z_size, kernel, focus_start, onset, freq_order):
    sds = jax.ShapeDtypeStruct
    _, n, rows, receivers = kernel.shape
    own, samples = focus_start.shape[0], focus_start.shape[2]
    n_f = freq_order.shape[0] // n
    points = n_f * own
    chips = 4 if n_f == 8 and own == 1 and n % 2 == 0 and z_size == 4 else 0
    place = lax.axis_index("rcv")[None].astype(jnp.int32)
    me = lax.axis_index("freq")[None].astype(jnp.int32)
    smem = pl.BlockSpec(memory_space=pltpu.SMEM)

    n_rows = 2 * freq_order.shape[0]
    traces = focus_start.reshape(own * rows, samples)

    def trade(x, d):
        return lax.ppermute(x, "freq", [(i, i ^ d) for i in range(n_f)])

    def across(pieces):
        moved = {q: trade(pieces[q], 2 * q) for q in (3, 1, 2)}
        return [pieces[0]] + [moved[q] for q in (1, 2, 3)]

    def from_hbm(*arrays):
        return [pltpu.with_memory_space_constraint(x, pltpu.HBM) for x in arrays]

    order, limit = freq_order.reshape(1, -1), onset.reshape(1, -1)
    order_scratch = pltpu.VMEM((1, n_rows // 2), jnp.int32)
    if chips:
        given = trade(traces, 1)
        other = trade(limit, 1)
        *table, scale, near_limit, local = call(
            functools.partial(pair_table_body, chips, n),
            [HBM] * 3 + [smem],
            [sds((n_rows // 2, samples), BF16)] * 2
            + [sds((samples, n_rows), BF16)] * 2
            + [sds((n_rows, 1), F32), sds((1, rows), jnp.int32), sds((rows, samples), F32)],
            [*from_hbm(order, limit, traces), me],
            scratch=[order_scratch, pltpu.SemaphoreType.DMA((3,))],
        )
        limit, *start = call(
            pair_spectrum_body,
            [VMEM] * 6,
            [sds((1, 2 * rows), jnp.int32)] + [sds((2, 2 * n, rows), F32)] * chips,
            (*table[:2], local, given, near_limit, other),
        )
    else:
        *table, scale, limit, start = call(
            functools.partial(spectrum_body, n),
            [HBM] * 3,
            [sds((n_rows, samples), BF16)] * 2
            + [sds((n_rows, 1), F32), sds((own * rows, 1), jnp.int32)]
            + [sds((n_rows, own * rows), F32)],
            from_hbm(order, limit, traces),
            scratch=[
                order_scratch,
                pltpu.VMEM((1, own * rows), jnp.int32),
                pltpu.VMEM((own * rows, samples), F32),
                pltpu.SemaphoreType.DMA((3,)),
            ],
        )

    held = None

    def shift(x, d):
        return lax.ppermute(x, "rcv", [(i, i ^ d) for i in range(z_size)])

    def gather(near, x, low=None, high=None):
        if z_size != 4 or n % 2 or held is None:
            far = {d: shift(x, d) for d in range(1, z_size)}
            pieces = [(0, 0, x)] + [(d, 0, far[d]) for d in far]
        else:
            half = n // 2
            b0 = shift(low, 2)
            a = shift(x, 1)
            c1 = shift(high, 3)
            b1 = shift(high, 2)
            c0 = shift(b0, 1)
            pieces = [(0, 0, x), (2, 0, b0), (3, half, c1), (1, 0, a), (2, half, b1), (3, 0, c0)]
        return [
            [(b, at, [near[b], array] if near else [array])] for b, at, array in pieces
        ]

    def field_scratch(arrays):
        if len(arrays) == 1:
            return []
        return [pltpu.VMEM((arrays[1].shape[1] // 2, 2, points, rows), F32)]

    def hold(arrays, parity):
        shape = (2, n, rows, rows)
        *outs, total = pl.pallas_call(
            functools.partial(hold_body, z_size, parity, len(arrays)),
            in_specs=[HBM, smem] + [VMEM] * len(arrays),
            out_specs=(VMEM,) * (2 * z_size + 1),
            out_shape=(pltpu.VMEM(shape, BF16),) * (2 * z_size)
            + (sds((n, 2, points, rows), F32),),
            scratch_shapes=[pltpu.VMEM((6, 2, rows, receivers), F32), pltpu.SemaphoreType.DMA((6,))]
            + field_scratch(arrays),
            compiler_params=pltpu.CompilerParams(vmem_limit_bytes=16 << 20),
        )(kernel, place, *arrays)
        return outs, [total]

    def product(spectrum, parity):
        nonlocal held
        if chips:
            pieces = across(spectrum)
            near = [pieces[0]] + [shift(pieces[0], d) for d in range(1, z_size)]
            far = points - 2
            shapes = [(far, 2 * n, rows)] + ([(far, n, rows)] * 2 if held else [])
            packed = call(
                functools.partial(pack_body, chips - 1),
                [VMEM] * (chips - 1),
                [sds(shape, F32) for shape in shapes],
                pieces[1:],
            )
            groups = gather(near, *packed)
        else:
            s = spectrum.reshape(n_f, 2 * n, own, rows)
            x = lax.all_to_all(s, "freq", split_axis=0, concat_axis=0, tiled=True)
            x = x.reshape(n_f, n, 2, own, rows).transpose(1, 2, 0, 3, 4)
            x = x.reshape(n, 2, points, rows)
            groups = gather(None, x, x[: n // 2], x[n // 2 :])
        total = None
        if held is None:
            held, total = hold(groups.pop(0)[0][2], parity)
        for step, group in enumerate(groups):
            args = [held[2 * b + h] for h in (0, 1) for b, _, _ in group]
            widths = [len(arrays) for _, _, arrays in group]
            args += [x for _, _, arrays in group for x in arrays]
            scratch = [x for _, _, arrays in group for x in field_scratch(arrays)]
            first, end = total is None, chips if step == len(groups) - 1 else 0
            outs = [sds((2, 2 * n, rows), F32)] * end or [sds((n, 2, points, rows), F32)]
            if not first:
                args += total
            pieces = [piece[:2] for piece in group]
            total = call(
                functools.partial(product_body, parity, pieces, first, end, widths),
                [VMEM] * len(args),
                outs,
                args,
                scratch=scratch,
                alias=None if first or end else {len(args) - 1: 0},
            )
        if chips:
            back = across(total)
            return back + [trade(x, 1) for x in back]
        back = total[0].reshape(2 * n, n_f, own, rows).transpose(1, 0, 2, 3)
        back = lax.all_to_all(back, "freq", split_axis=0, concat_axis=0, tiled=True)
        return back.reshape(n_rows, own * rows)

    def mute(back, last, base):
        if chips:
            base = [] if base is None else [base] if last else base
            outs = [sds((rows, samples), F32)] if last else [sds((2, 2 * n, rows), F32)] * chips
            args = (scale, limit, *table, *back, *base)
            body = functools.partial(pair_mute_body, chips, last, len(base))
            got = call(body, [VMEM] * len(args), outs, args)
            return got[0] if last else got
        outs = [sds((own * rows, samples) if last else (n_rows, own * rows), F32)]
        args = (scale, limit, back, *table) + (() if base is None else (base,))
        body = functools.partial(mute_body, last, base is not None)
        return call(body, [VMEM] * len(args), outs, args)[0]

    field = start
    for iteration in range(ITERS):
        final = iteration == ITERS - 1
        back = product(field, 1.0)
        field = mute(back, False, None)
        if final:
            downgoing = mute(back, True, None)
        back = product(field, -1.0)
        field = mute(back, final, traces if final else start)
    return field.reshape(focus_start.shape), downgoing.reshape(focus_start.shape)


def solution(mesh):
    in_specs = (P(None, "freq", "rcv", None), P("freq", "rcv", None), P("freq", "rcv"), P())
    out_specs = (P("freq", "rcv", None), P("freq", "rcv", None))
    return jax.shard_map(
        functools.partial(body, mesh.shape["rcv"]),
        mesh=mesh,
        in_specs=in_specs,
        out_specs=out_specs,
        check_vma=False,
    )
```
